256 devices in a mesh: rows: 32 (over y, x, core), cols: 8 (over z).
Axes of the slice: x: 4, y: 4, z: 8, core: 2. Of those that a mesh axis runs over, the one named last changes fastest.
Arguments:
- owner_map: int32 [2, 512], replicated, may hold values from 0 to 511, as said below
- colidx: int32 [2, 512, 24], P(None, 'rows', 'cols'), may hold values from 0 to 767, as said below
- live: int32 [2, 512], P(None, 'rows'), may hold values from 1 to 24
- blocks: bfloat16 [2, 512, 24, 128, 128], P(None, 'rows', 'cols'), may hold values from -0.15625 to 0.15625
- diag_inverse: float32 [2, 512, 128, 128], P(None, 'rows')
- right_side: float32 [2, 512, 64, 128], P(None, 'rows'), may hold values from -6 to 6
- prior: bfloat16 [256, 64, 128], P('rows'), may hold values from -6 to 6
Outputs:
- solved: float32 [2, 512, 64, 128], P(None, 'rows')
The draws below stay inside these ranges and needn't reach their ends.
Inputs may be any that keep to these rules, and one draw needn't show every extreme that they name: Each row of owner_map is a permutation of the block rows of a front. `colidx`: front 0 refers only to earlier block rows; in front 1, even slots refer to rows of front 0 and odd slots to earlier block rows. Take the even slots of front 1 that lie in block rows s with s // 16 equal to one value and in slots j with j // 3 equal to one value. Among them, at most 1 refer to front-0 rows r whose slot t (owner_map[0, t] = r) has t // 16 equal to any single value; some such group reaches 1.
All inputs are finite; a program needn't handle non-finite values.
Results may differ from the reference program's by a relative error of at most 0.0017.
Values may be sent and summed in bfloat16 or wider, within the bound.
A program may use at most 64 MiB of HBM per device.

```python
import jax
import jax.numpy as jnp
from jax import lax

B = 128
P_SIZE = 64
NB = 24
ROWS_DEV = 16
ROWS_F = 512
NPRI = 256
NBC = 3
CAP = 1


def draw_owner_map(key, part):
    first = jax.random.permutation(jax.random.fold_in(key, 11), ROWS_F)
    second = jax.random.permutation(jax.random.fold_in(key, 12), ROWS_F)
    row_groups = ROWS_F // ROWS_DEV
    col_groups = NB // NBC
    per_block = ROWS_DEV * NBC
    shift = jax.random.randint(jax.random.fold_in(key, 25), (row_groups, col_groups, 1), 0, row_groups)
    within = jax.random.randint(jax.random.fold_in(key, 26), (row_groups, col_groups, per_block), 0, ROWS_DEV)
    target = shift[0, 0, 0] * ROWS_DEV + within[0, 0, 0]
    held = first[target]
    where_top = jnp.argmax(first == ROWS_F - 1)
    first = first.at[where_top].set(held).at[target].set(ROWS_F - 1)
    return jnp.stack([first, second]).astype(jnp.int32)


def draw_colidx(key, part):
    owner_map = draw_owner_map(key, part)
    early_a = jax.random.randint(jax.random.fold_in(key, 21), (ROWS_F, NB), 0, NPRI)
    early_b = jax.random.randint(jax.random.fold_in(key, 22), (ROWS_F, NB), 0, NPRI)
    row_groups = ROWS_F // ROWS_DEV
    col_groups = NB // NBC
    per_block = ROWS_DEV * NBC
    spread = row_groups * CAP
    slot_ids = jnp.arange(col_groups)[:, None, None] * NBC + jnp.arange(NBC)[None, None, :]
    even = jnp.broadcast_to(slot_ids % 2 == 0, (col_groups, ROWS_DEV, NBC)).reshape(col_groups, per_block)
    rank = jnp.clip(jnp.cumsum(even.astype(jnp.int32), axis=-1) - 1, 0, spread - 1)
    scores = jax.random.randint(jax.random.fold_in(key, 24), (row_groups, col_groups, spread), 0, 65536)
    scores = scores * spread + jnp.arange(spread)
    scores = jnp.where(jnp.arange(spread) < CAP, jnp.arange(spread) - CAP, scores)
    order = jnp.argsort(scores, axis=-1)
    rank_all = jnp.broadcast_to(rank[None], (row_groups, col_groups, per_block))
    holders = jnp.take_along_axis(order, rank_all, axis=-1) // CAP
    shift = jax.random.randint(jax.random.fold_in(key, 25), (row_groups, col_groups, 1), 0, row_groups)
    holders = (holders + shift) % row_groups
    within = jax.random.randint(jax.random.fold_in(key, 26), (row_groups, col_groups, per_block), 0, ROWS_DEV)
    recent = NPRI + owner_map[0][holders * ROWS_DEV + within]
    recent = recent.reshape(row_groups, col_groups, ROWS_DEV, NBC).transpose(0, 2, 1, 3).reshape(ROWS_F, NB)
    even_full = jnp.broadcast_to((jnp.arange(NB) % 2 == 0)[None, :], (ROWS_F, NB))
    second = jnp.where(even_full, recent, early_b)
    early_a = early_a.at[0, 0].set(0)
    return jnp.stack([early_a, second]).astype(jnp.int32)


def draw_live(key, part):
    counts = jax.random.randint(jax.random.fold_in(key, 31), (2, ROWS_F), 1, NB + 1)
    pick = jax.random.randint(jax.random.fold_in(key, 32), (2, ROWS_F), 0, 4)
    counts = jnp.where(pick == 0, NB, counts)
    counts = counts.at[:, 0].set(NB).at[:, 1].set(1)
    return counts.astype(jnp.int32)


def draw_diag_inverse(key, part):
    eye = jnp.eye(B, dtype=jnp.float32)
    diag = jax.random.uniform(jax.random.fold_in(key, 41), (2, ROWS_F, 1, B), jnp.float32, 0.8, 1.2)
    rest = 0.05 * jax.random.normal(jax.random.fold_in(key, 42), (2, ROWS_F, B, B), jnp.float32)
    return (eye * diag + rest).astype(jnp.float32)


def block_levels(stream_key, extent, shards, least, high):
    def one(position, blocks):
        draws = jax.random.uniform(jax.random.fold_in(jax.random.fold_in(stream_key, 6), position), (blocks,), jnp.float32, least / len(shards), high / len(shards))
        return jnp.repeat(jnp.exp(draws), extent[position] // blocks).reshape((-1,) + (1,) * (len(extent) - position - 1))

    loudness = one(*shards[0])
    for cut in shards[1:]:
        loudness = loudness * one(*cut)
    return loudness


def normal_values(own_key, extent, scale, limit, pieces=(), kind=jnp.bfloat16):
    array = jax.random.normal(own_key, extent, jnp.float32) * scale
    if len(pieces) > 0:
        array = block_levels(own_key, extent, pieces, -0.22, 0.18) * array
    return jnp.clip(array, min=-limit, max=limit).astype(kind)


def setup_inputs(seed: int = 0) -> dict:
    key_list = jax.random.split(jax.random.key(seed), 8)
    return {
        "owner_map": draw_owner_map(jax.random.fold_in(key_list[7], 71), 0),
        "colidx": draw_colidx(jax.random.fold_in(key_list[7], 71), 0),
        "live": draw_live(jax.random.fold_in(key_list[7], 71), 0),
        "blocks": normal_values(key_list[3], (2, ROWS_F, NB, B, B), (B * NB // 2) ** -0.5, 0.15625, ((1, 32), (2, 8))),
        "diag_inverse": draw_diag_inverse(jax.random.fold_in(key_list[7], 71), 0),
        "right_side": normal_values(key_list[5], (2, ROWS_F, P_SIZE, B), 1.0, 6.0, ((1, 32),), jnp.float32),
        "prior": normal_values(key_list[6], (NPRI, P_SIZE, B), 1.0, 6.0, ((0, 32),)),
    }


def solve_front(front, known, colidx, live, blocks, diag_inverse, right_side):
    slots = jnp.arange(NB)
    mask = slots[None, :] < live[front][:, None]

    def one_row(items):
        blk, idx, keep, rhs, inverse = items
        xs = jnp.where(keep[:, None, None], known[idx], jnp.zeros((), known.dtype)).astype(jnp.float32)
        total = jnp.einsum("jcb,jpb->pc", blk.astype(jnp.float32), xs)
        resid = rhs - total
        return jnp.einsum("pb,cb->pc", resid, inverse, precision=lax.Precision.HIGHEST)

    return lax.map(one_row, (blocks[front], colidx[front], mask, right_side[front], diag_inverse[front]))


def reference(owner_map, colidx, live, blocks, diag_inverse, right_side, prior):
    first = solve_front(0, prior, colidx, live, blocks, diag_inverse, right_side)
    placed = jnp.zeros_like(first).at[owner_map[0]].set(first).astype(jnp.bfloat16)
    known = jnp.concatenate([prior, placed], axis=0)
    second = solve_front(1, known, colidx, live, blocks, diag_inverse, right_side)
    return jnp.stack([first, second])
```

```python
import functools

import jax
import jax.numpy as jnp
from jax import lax
from jax.experimental import pallas as pl
from jax.experimental.pallas import tpu as pltpu
from jax.sharding import PartitionSpec as P

MESH = pl.DeviceIdType.MESH
NX, NY, NCORE, NZ = 4, 4, 2, 8
NR = NX * NY * NCORE
PRI_DEV = 8
NPRI = NR * PRI_DEV
ROWS_DEV = 16
SEG = ROWS_DEV // NZ
NBC = 3
P_SIZE, B = 64, 128
NT = (((1,), (1,)), ((), ()))
ORDER = (4, 3, 5, 2, 6, 1, 7, 0)


def kernel(
    tbl, want, blocks, dinv, rhs, prior, out,
    known, recent, blk, dv, rh, part, rs, sol, low, a2a, want_in, sel,
    loc_sem, out_sem, w_s, w_r, t_s, t_r, sib_s, sib_r, rs_s, rs_r, ag_s, ag_r, a_s, a_r,
):
    r = lax.axis_index("rows")
    c = lax.axis_index("cols")
    core = lax.rem(r, 2)
    cx = lax.rem(r // 2, NX)
    cy = r // (2 * NX)

    def rid(y, x, k):
        return (lax.rem(y + NY, NY) * NX + lax.rem(x + NX, NX)) * 2 + k

    def remote(src, dst, ss, rr, dev):
        return pltpu.make_async_remote_copy(
            src_ref=src, dst_ref=dst, send_sem=ss, recv_sem=rr, device_id=dev, device_id_type=MESH
        )

    own = known.at[pl.ds(r * PRI_DEV, PRI_DEV)]
    ld_prior = pltpu.make_async_copy(prior, own, loc_sem.at[0])
    ld_blk = pltpu.make_async_copy(blocks, blk, loc_sem.at[1])
    ld_dv = pltpu.make_async_copy(dinv.at[:, pl.ds(c * SEG, SEG)], dv, loc_sem.at[2])
    ld_rh = pltpu.make_async_copy(rhs.at[:, pl.ds(c * SEG, SEG)], rh, loc_sem.at[3])
    ld_prior.start()
    ld_blk.start()
    ld_dv.start()
    ld_rh.start()
    known[NPRI] = jnp.zeros((P_SIZE, B), jnp.bfloat16)
    recent[NR] = jnp.zeros((P_SIZE, B), jnp.bfloat16)

    barrier = pltpu.get_barrier_semaphore()

    def greet_rows(e, carry):
        pl.semaphore_signal(barrier, inc=1, device_id=(lax.rem(r + e, NR), c), device_id_type=MESH)
        return carry

    def greet_cols(e, carry):
        pl.semaphore_signal(barrier, inc=1, device_id=(r, lax.rem(c + e, NZ)), device_id_type=MESH)
        return carry

    lax.fori_loop(1, NR, greet_rows, 0)
    lax.fori_loop(1, NZ, greet_cols, 0)
    pl.semaphore_wait(barrier, NR - 1 + NZ - 1)
    ld_prior.wait()

    sends = []

    def src_rows(h, du, dv_, lo, n):
        x, y = (cx - du, cy - dv_) if h == 0 else (cx - dv_, cy - du)
        base = rid(y + NY, x + NX, core) * PRI_DEV + h * 4 + lo
        return known.at[pl.ds(base, n)]

    def neighbour(h, du, dv_):
        x, y = (cx + du, cy + dv_) if h == 0 else (cx + dv_, cy + du)
        return (rid(y + NY, x + NX, core), c)

    sem_of = {}

    def recv_id(h, du, dv_, q):
        return h * 32 + ((du + 4) % 4) * 8 + ((dv_ + 4) % 4) * 2 + q

    def push(h, item, step, lo, n, q):
        rows = src_rows(h, item[0], item[1], lo, n)
        got = recv_id(h, item[0] + step[0], item[1] + step[1], q)
        i = len(sends)
        cp = remote(rows, rows, t_s.at[i], t_r.at[got], neighbour(h, *step))
        cp.start()
        sends.append(cp)

    def arrive(h, item, lo, n, q):
        rows = src_rows(h, item[0], item[1], lo, n)
        got = recv_id(h, item[0], item[1], q)
        remote(rows, rows, t_s.at[0], t_r.at[got], (r, c)).wait_recv()

    sib = []

    def to_sibling(h, item):
        rows = src_rows(h, item[0], item[1], 0, 4)
        i = len(sib)
        j = h * 16 + ((item[0] + 4) % 4) * 4 + ((item[1] + 4) % 4)
        cp = remote(rows, rows, sib_s.at[i], sib_r.at[j], (rid(cy + NY, cx + NX, 1 - core), c))
        cp.start()
        sib.append((cp, h, item, j))

    def spread(h, item):
        push(h, item, (0, 1), 0, 4, 0)
        push(h, item, (0, -1), 0, 4, 0)

    for h in (0, 1):
        push(h, (0, 0), (1, 0), 0, 4, 0)
        push(h, (0, 0), (-1, 0), 0, 4, 0)
    for h in (0, 1):
        spread(h, (0, 0))
        to_sibling(h, (0, 0))
    for h in (0, 1):
        arrive(h, (1, 0), 0, 4, 0)
        push(h, (1, 0), (1, 0), 0, 2, 0)
        arrive(h, (-1, 0), 0, 4, 0)
        push(h, (-1, 0), (-1, 0), 2, 2, 1)
        for du in (1, -1):
            spread(h, (du, 0))
            to_sibling(h, (du, 0))

    def ask(e, carry):
        peer = lax.rem(r + e, NR)
        remote(want.at[peer], want_in.at[r], w_s.at[e], w_r.at[e], (peer, c)).start()
        return carry

    lax.fori_loop(1, NR, ask, 0)
    keep_own = pltpu.make_async_copy(want.at[r], want_in.at[r], loc_sem.at[4])
    keep_own.start()

    def second(h, du):
        arrive(h, (du, 1), 0, 4, 0)
        push(h, (du, 1), (0, 1), 0, 2, 0)
        to_sibling(h, (du, 1))
        arrive(h, (du, -1), 0, 4, 0)
        push(h, (du, -1), (0, -1), 2, 2, 1)
        to_sibling(h, (du, -1))

    def far(h, du, dv_):
        if du == 2 and dv_ == 0:
            arrive(h, (2, 0), 0, 2, 0)
            arrive(h, (2, 0), 2, 2, 1)
        else:
            arrive(h, (du, 2), 0, 2, 0)
            arrive(h, (du, 2), 2, 2, 1)
        to_sibling(h, (du, dv_))

    for h in (0, 1):
        second(h, 0)
    for h in (0, 1):
        far(h, 2, 0)
        spread(h, (2, 0))
    for du in (1, -1):
        for h in (0, 1):
            second(h, du)
    for h in (0, 1):
        far(h, 0, 2)
    for h in (0, 1):
        second(h, 2)
    for du in (1, -1, 2):
        for h in (0, 1):
            far(h, du, 2)
    for cp, h, item, j in sib:
        x, y = (cx - item[0], cy - item[1]) if h == 0 else (cx - item[1], cy - item[0])
        base = rid(y + NY, x + NX, 1 - core) * PRI_DEV + h * 4
        rows = known.at[pl.ds(base, 4)]
        remote(rows, rows, sib_s.at[0], sib_r.at[j], (r, c)).wait_recv()
    ld_blk.wait()

    def product(f, s, held, slots):
        xs = jnp.concatenate([held[tbl[f, s * NBC + j]] for j in slots], axis=1)
        ws = jnp.concatenate([blk[f, s, j] for j in slots], axis=1)
        return lax.dot_general(xs, ws, NT, preferred_element_type=jnp.float32)

    def rows_of(peer, body):
        def one(q, carry):
            body(peer * SEG + q)
            return carry

        lax.fori_loop(0, SEG, one, 0)

    def scatter(f, d, peer):
        remote(
            part.at[f, pl.ds(peer * SEG, SEG)], rs.at[f, d], rs_s.at[f, d], rs_r.at[f, d], (r, peer)
        ).start()

    def first_products():
        for d in ORDER:
            peer = lax.rem(c + d, NZ)

            def body(s):
                part[0, s] = product(0, s, known, (0, 1, 2))

            rows_of(peer, body)
            if d != 0:
                scatter(0, d, peer)

    even_col = lax.rem(c, 2) == 0

    def early_products():
        def step(slots):
            def one(s, carry):
                part[1, s] = product(1, s, known, slots)
                return carry

            lax.fori_loop(0, ROWS_DEV, one, 0)

        pl.when(even_col)(lambda: step((1,)))
        pl.when(jnp.logical_not(even_col))(lambda: step((0, 2)))

    def late_products():
        for d in ORDER:
            peer = lax.rem(c + d, NZ)

            def step(slots):
                def body(s):
                    part[1, s] += product(1, s, recent, slots)

                rows_of(peer, body)

            pl.when(even_col)(lambda: step((0, 2)))
            pl.when(jnp.logical_not(even_col))(lambda: step((1,)))
            if d != 0:
                scatter(1, d, peer)

    def finish(f):
        for d in range(1, NZ):
            remote(
                part.at[f, pl.ds(0, SEG)], rs.at[f, d], rs_s.at[f, d], rs_r.at[f, d], (r, lax.rem(c + d, NZ))
            ).wait_recv()
        for q in range(SEG):
            total = part[f, c * SEG + q]
            for d in range(1, NZ):
                total = total + rs[f, d, q]
            sol[f, c * SEG + q] = lax.dot_general(
                rh[f, q] - total, dv[f, q], NT,
                precision=lax.Precision.HIGHEST, preferred_element_type=jnp.float32,
            )
        mine = sol.at[f, pl.ds(c * SEG, SEG)]
        for d in ORDER[:-1]:
            peer = lax.rem(c + d, NZ)
            remote(mine, mine, ag_s.at[f, d], ag_r.at[f, d], (r, peer)).start()
        for d in ORDER[:-1]:
            theirs = sol.at[f, pl.ds(lax.rem(c + NZ - d, NZ) * SEG, SEG)]
            remote(theirs, theirs, ag_s.at[f, d], ag_r.at[f, d], (r, c)).wait_recv()

    first_products()
    early_products()
    ld_dv.wait()
    ld_rh.wait()
    finish(0)

    def asked(e, carry):
        remote(want.at[0], want_in.at[lax.rem(r + NR - e, NR)], w_s.at[e], w_r.at[e], (r, c)).wait_recv()
        return carry

    lax.fori_loop(1, NR, asked, 0)
    keep_own.wait()
    to_scalar = pltpu.make_async_copy(want_in, sel, loc_sem.at[5])
    to_scalar.start()
    out0 = pltpu.make_async_copy(sol.at[0], out.at[0], out_sem.at[0])
    out0.start()

    def narrow(i, carry):
        low[i] = sol[0, i].astype(jnp.bfloat16)
        return carry

    lax.fori_loop(0, ROWS_DEV, narrow, 0)
    to_scalar.wait()

    def give(e, carry):
        peer = lax.rem(r + e, NR)
        a2a[e] = low[sel[peer, 0, 0]]
        remote(a2a.at[e], recent.at[r], a_s.at[e], a_r.at[e], (peer, c)).start()
        return carry

    lax.fori_loop(1, NR, give, 0)
    recent[r] = low[sel[r, 0, 0]]

    def take(e, carry):
        slot = recent.at[lax.rem(r + NR - e, NR)]
        remote(slot, slot, a_s.at[e], a_r.at[e], (r, c)).wait_recv()
        return carry

    lax.fori_loop(1, NR, take, 0)

    late_products()
    finish(1)
    out1 = pltpu.make_async_copy(sol.at[1], out.at[1], out_sem.at[1])
    out1.start()

    for cp in sends:
        cp.wait_send()
    for cp, h, item, j in sib:
        cp.wait_send()

    def left(e, carry):
        peer = lax.rem(r + e, NR)
        remote(want.at[peer], want_in.at[r], w_s.at[e], w_r.at[e], (peer, c)).wait_send()
        remote(a2a.at[e], recent.at[r], a_s.at[e], a_r.at[e], (peer, c)).wait_send()
        return carry

    lax.fori_loop(1, NR, left, 0)
    for f in (0, 1):
        mine = sol.at[f, pl.ds(c * SEG, SEG)]
        for d in range(1, NZ):
            peer = lax.rem(c + d, NZ)
            remote(
                part.at[f, pl.ds(peer * SEG, SEG)], rs.at[f, d], rs_s.at[f, d], rs_r.at[f, d], (r, peer)
            ).wait_send()
            remote(mine, mine, ag_s.at[f, d], ag_r.at[f, d], (r, peer)).wait_send()
    out0.wait()
    out1.wait()


def shards(owner_map, colidx, live, blocks, diag_inverse, right_side, prior):
    col_here = lax.axis_index("cols")
    slot_ids = col_here * NBC + jnp.arange(NBC, dtype=jnp.int32)
    live_mask = slot_ids[None, None, :] < live[:, :, None]
    rows_front = owner_map.shape[1]
    row = colidx[1].reshape(-1) - NPRI
    slots = jnp.arange(rows_front, dtype=jnp.int32)
    place = jnp.sum(jnp.where(row[:, None] == owner_map[0][None, :], slots[None, :], 0), axis=1)
    recent = row >= 0
    holder = jnp.where(recent, place // ROWS_DEV, -1)
    second = jnp.where(recent, holder, row + NPRI).reshape(ROWS_DEV, NBC)
    both = jnp.stack([colidx[0], second])
    empty = jnp.stack([jnp.full((ROWS_DEV * NBC,), NPRI), jnp.where(recent, NR, NPRI)]).reshape(2, ROWS_DEV, NBC)
    tbl = jnp.where(live_mask, both, empty).reshape(2, ROWS_DEV * NBC)
    want = jnp.max(
        jnp.where(jnp.arange(NR, dtype=jnp.int32)[:, None] == holder[None, :], (place % ROWS_DEV)[None, :], 0), axis=1
    )
    want = jnp.broadcast_to(want[:, None, None], (NR, 1, B))
    dma = pltpu.SemaphoreType.DMA
    any_spec = pl.BlockSpec(memory_space=pl.ANY)
    return pl.pallas_call(
        kernel,
        out_shape=jax.ShapeDtypeStruct((2, ROWS_DEV, P_SIZE, B), jnp.float32),
        in_specs=[
            pl.BlockSpec(memory_space=pltpu.SMEM),
            pl.BlockSpec(memory_space=pltpu.VMEM),
            any_spec, any_spec, any_spec, any_spec,
        ],
        out_specs=any_spec,
        scratch_shapes=[
            pltpu.VMEM((NPRI + 1, P_SIZE, B), jnp.bfloat16),
            pltpu.VMEM((NR + 1, P_SIZE, B), jnp.bfloat16),
            pltpu.VMEM((2, ROWS_DEV, NBC, B, B), jnp.bfloat16),
            pltpu.VMEM((2, SEG, B, B), jnp.float32),
            pltpu.VMEM((2, SEG, P_SIZE, B), jnp.float32),
            pltpu.VMEM((2, ROWS_DEV, P_SIZE, B), jnp.float32),
            pltpu.VMEM((2, NZ, SEG, P_SIZE, B), jnp.float32),
            pltpu.VMEM((2, ROWS_DEV, P_SIZE, B), jnp.float32),
            pltpu.VMEM((ROWS_DEV, P_SIZE, B), jnp.bfloat16),
            pltpu.VMEM((NR, P_SIZE, B), jnp.bfloat16),
            pltpu.VMEM((NR, 1, B), jnp.int32),
            pltpu.SMEM((NR, 1, B), jnp.int32),
            dma((6,)), dma((2,)),
            dma((NR,)), dma((NR,)),
            dma((40,)), dma((64,)),
            dma((32,)), dma((32,)),
            dma((2, NZ)), dma((2, NZ)),
            dma((2, NZ)), dma((2, NZ)),
            dma((NR,)), dma((NR,)),
        ],
        compiler_params=pltpu.CompilerParams(
            collective_id=0, has_side_effects=True, vmem_limit_bytes=40 * 1024 * 1024
        ),
    )(tbl, want, blocks, diag_inverse, right_side, prior)


def solution(mesh):
    placed = (
        P(),
        P(None, "rows", "cols"),
        P(None, "rows"),
        P(None, "rows", "cols", None, None),
        P(None, "rows", None, None),
        P(None, "rows", None, None),
        P("rows", None, None),
    )
    return jax.shard_map(
        shards, mesh=mesh, in_specs=placed, out_specs=P(None, "rows", None, None), check_vma=False
    )
```

```python
import jax
import jax.numpy as jnp
from jax import lax
from jax.experimental import pallas as pl
from jax.experimental.pallas import tpu as pltpu
from jax.sharding import PartitionSpec as P

MESH = pl.DeviceIdType.MESH
NX, NY, NZ = 4, 4, 8
NR = NX * NY * 2
PRI_DEV = 8
HALF = PRI_DEV // 2
NPRI = NR * PRI_DEV
ROWS_DEV = 16
ROWS_F = NR * ROWS_DEV
SEG = ROWS_DEV // NZ
NBC = 3
SLOTS = ROWS_DEV * NBC
P_SIZE, B = 64, 128
SEG_ROWS = SEG * P_SIZE
CODED = SEG_ROWS + 16
NT = (((1,), (1,)), ((), ()))
PEERS = (4, 3, 5, 2, 6, 1, 7)


def encode(value):
    top = jnp.maximum(jnp.max(jnp.abs(value), axis=0, keepdims=True), 1e-30)
    power = jnp.ceil(jnp.log2(top) + 0.01)
    fixed = jnp.round(value * jnp.exp2(15.0 - power)).astype(jnp.int32).astype(jnp.int16)
    powers = jnp.broadcast_to(power, (16, B)).astype(jnp.int32).astype(jnp.int16)
    return fixed, powers


def decode(fixed, powers):
    unit = jnp.exp2(powers.astype(jnp.int32).astype(jnp.float32) - 15.0)
    value = fixed.astype(jnp.int32).astype(jnp.float32).reshape(SEG_ROWS // 16, 16, B) * unit[None]
    return value.reshape(SEG_ROWS, B)


def kernel(
    owners, cols, live, blocks, dinv, rhs, prior, out,
    known, recent, blk, dv, rh, part, own, code_s, code_r, fin, low, rest, a2a,
    om, place, want, want_in, col_s, live_s, place_s, sel,
    loc_sem, w_s, w_r, t_s, t_r, sib_s, sib_r, rs_s, rs_r, hi_s, hi_r, lo_s, lo_r, fin_s, fin_r, a_s, a_r,
):
    r = lax.axis_index("rows")
    c = lax.axis_index("cols")
    core = lax.rem(r, 2)
    cx = lax.rem(r // 2, NX)
    cy = r // (2 * NX)

    def rid(y, x, k):
        return (lax.rem(y + 2 * NY, NY) * NX + lax.rem(x + 2 * NX, NX)) * 2 + k

    def remote(src, dst, ss, rr, dev):
        return pltpu.make_async_remote_copy(
            src_ref=src, dst_ref=dst, send_sem=ss, recv_sem=rr, device_id=dev, device_id_type=MESH
        )

    locals_ = [
        pltpu.make_async_copy(src, dst, loc_sem.at[i])
        for i, (src, dst) in enumerate((
            (prior, known.at[pl.ds(r * PRI_DEV, PRI_DEV)]),
            (cols, col_s),
            (owners, om),
            (live, live_s),
            (blocks, blk),
            (dinv.at[:, pl.ds(c * SEG, SEG)], dv),
            (rhs.at[:, pl.ds(c * SEG, SEG)], rh),
        ))
    ]
    for cp in locals_:
        cp.start()
    ld_prior, ld_cols, ld_owners, ld_live, ld_blk, ld_dv, ld_rh = locals_

    barrier = pltpu.get_barrier_semaphore()

    def greet_rows(e, carry):
        pl.semaphore_signal(barrier, inc=1, device_id=(lax.rem(r + e, NR), c), device_id_type=MESH)
        return carry

    def greet_cols(e, carry):
        pl.semaphore_signal(barrier, inc=1, device_id=(r, lax.rem(c + e, NZ)), device_id_type=MESH)
        return carry

    lax.fori_loop(1, NR, greet_rows, 0)
    lax.fori_loop(1, NZ, greet_cols, 0)

    known[NPRI] = jnp.zeros((P_SIZE, B), jnp.bfloat16)
    recent[NR] = jnp.zeros((P_SIZE, B), jnp.bfloat16)

    ld_cols.wait()
    ld_owners.wait()
    ld_live.wait()
    ids = om[0:1, :]
    spots = lax.broadcasted_iota(jnp.int32, (1, ROWS_F), 1)

    def find(s, carry):
        for j in range(NBC):
            row = col_s[j, 1, s] - NPRI
            at = jnp.sum(jnp.where(ids == row, spots + 1, 0), axis=1, keepdims=True)
            place[s * NBC + j] = jnp.broadcast_to(at - 1, (1, B))
        return carry

    lax.fori_loop(0, ROWS_DEV, find, 0)
    to_place = pltpu.make_async_copy(place, place_s, loc_sem.at[7])
    to_place.start()
    lanes = lax.broadcasted_iota(jnp.int32, (SLOTS, 1, B), 2)
    spot = place[...]
    want[...] = jnp.max(jnp.where((spot >> 4) == lanes, spot & 15, 0), axis=0)
    pl.semaphore_wait(barrier, NR - 1 + NZ - 1)
    ld_prior.wait()

    sends = []

    def xy(h, a, b):
        return (a, b) if h == 0 else (b, a)

    def src_rows(h, item, lo, n, k):
        dx, dy = xy(h, *item)
        return known.at[pl.ds(rid(cy - dy, cx - dx, k) * PRI_DEV + h * HALF + lo, n)]

    def recv_id(h, item, q):
        return h * 32 + ((item[0] + 4) % 4) * 8 + ((item[1] + 4) % 4) * 2 + q

    def push(h, item, step, lo=0, n=HALF, q=0):
        rows = src_rows(h, item, lo, n, core)
        dx, dy = xy(h, *step)
        got = recv_id(h, (item[0] + step[0], item[1] + step[1]), q)
        cp = remote(rows, rows, t_s.at[len(sends)], t_r.at[got], (rid(cy + dy, cx + dx, core), c))
        cp.start()
        sends.append(cp)

    def arrive(h, item, lo=0, n=HALF, q=0):
        rows = src_rows(h, item, lo, n, core)
        remote(rows, rows, t_s.at[0], t_r.at[recv_id(h, item, q)], (r, c)).wait_recv()

    sib = []

    def to_sibling(h, item):
        rows = src_rows(h, item, 0, HALF, core)
        i = len(sib)
        cp = remote(rows, rows, sib_s.at[i], sib_r.at[i], (rid(cy, cx, 1 - core), c))
        cp.start()
        sib.append((cp, h, item))

    def spread(h, item):
        push(h, item, (0, 1))
        push(h, item, (0, -1))

    for h in (0, 1):
        push(h, (0, 0), (1, 0))
        push(h, (0, 0), (-1, 0))
    for h in (0, 1):
        push(h, (0, 0), (2, 0))
        spread(h, (0, 0))
    for h in (0, 1):
        to_sibling(h, (0, 0))

    def ask(e, carry):
        peer = lax.rem(r + e, NR)
        remote(want, want_in.at[r], w_s.at[e], w_r.at[e], (peer, c)).start()
        return carry

    lax.fori_loop(1, NR, ask, 0)
    keep_own = pltpu.make_async_copy(want, want_in.at[r], loc_sem.at[8])
    keep_own.start()

    for du in (1, -1):
        for h in (0, 1):
            arrive(h, (du, 0))
            spread(h, (du, 0))
            to_sibling(h, (du, 0))

    def relay(h, du):
        for dv_, lo, q in ((1, 0, 0), (-1, HALF // 2, 1)):
            arrive(h, (du, dv_))
            push(h, (du, dv_), (0, dv_), lo, HALF // 2, q)
            to_sibling(h, (du, dv_))

    for h in (0, 1):
        arrive(h, (2, 0))
        spread(h, (2, 0))
        push(h, (2, 0), (0, 2))
        to_sibling(h, (2, 0))
    for du in (0, 1, -1):
        for h in (0, 1):
            relay(h, du)
    for du in (0, 1, -1):
        for h in (0, 1):
            for q in (0, 1):
                arrive(h, (du, 2), q * HALF // 2, HALF // 2, q)
            to_sibling(h, (du, 2))
    for dv_ in (1, -1, 2):
        for h in (0, 1):
            arrive(h, (2, dv_))
            to_sibling(h, (2, dv_))
    ld_blk.wait()
    for i, (cp, h, item) in enumerate(sib):
        rows = src_rows(h, item, 0, HALF, 1 - core)
        remote(rows, rows, sib_s.at[0], sib_r.at[i], (r, c)).wait_recv()

    def product(f, s, held, index, slots):
        xs = jnp.concatenate([held[index(s, j)] for j in slots], axis=1)
        ws = jnp.concatenate([blk[f, s, j] for j in slots], axis=1)
        return lax.dot_general(xs, ws, NT, preferred_element_type=jnp.float32)

    def old_index(f):
        return lambda s, j: jnp.where(c * NBC + j < live_s[f, s], col_s[j, f, s], NPRI)

    def new_index(s, j):
        return jnp.where(c * NBC + j < live_s[1, s], place_s[s * NBC + j, 0, 0] >> 4, NR)

    def code_copy(f, d):
        return remote(
            code_s.at[f, d], code_r.at[f, d], rs_s.at[f, d], rs_r.at[f, d], (r, lax.rem(c + d, NZ))
        )

    def put(ref, value):
        fixed, powers = encode(value)
        ref[0:SEG_ROWS] = fixed
        ref[SEG_ROWS:CODED] = powers

    def scatter(f, row):
        for d in PEERS:
            peer = lax.rem(c + d, NZ)
            put(code_s.at[f, d], jnp.concatenate([row(peer * SEG + q) for q in range(SEG)], axis=0))
            code_copy(f, d).start()
        for q in range(SEG):
            own[f, q] = row(c * SEG + q)

    def solve(f):
        total = own[f].reshape(SEG_ROWS, B)
        for d in PEERS:
            code_copy(f, d).wait_recv()
            total = total + decode(code_r[f, d, 0:SEG_ROWS], code_r[f, d, SEG_ROWS:CODED])
        return [
            lax.dot_general(
                rh[f, q] - total[q * P_SIZE : (q + 1) * P_SIZE], dv[f, q], NT,
                precision=lax.Precision.HIGHEST, preferred_element_type=jnp.float32,
            )
            for q in range(SEG)
        ]

    def to_cols(ref, ss, rr, size):
        mine = ref.at[pl.ds(c * size, size)]
        return [remote(mine, mine, ss.at[d], rr.at[d], (r, lax.rem(c + d, NZ))) for d in PEERS]

    def from_cols(ref, ss, rr, size, d):
        theirs = ref.at[pl.ds(lax.rem(c + NZ - d, NZ) * size, size)]
        remote(theirs, theirs, ss.at[d], rr.at[d], (r, c)).wait_recv()

    scatter(0, lambda s: product(0, s, known, old_index(0), (0, 1, 2)))

    even_col = lax.rem(c, 2) == 0

    def early(slots):
        def one(s, carry):
            part[s] = product(1, s, known, old_index(1), slots)
            return carry

        lax.fori_loop(0, ROWS_DEV, one, 0)

    pl.when(even_col)(lambda: early((1,)))
    pl.when(jnp.logical_not(even_col))(lambda: early((0, 2)))

    def asked(e, carry):
        remote(want, want_in.at[lax.rem(r + NR - e, NR)], w_s.at[e], w_r.at[e], (r, c)).wait_recv()
        return carry

    lax.fori_loop(1, NR, asked, 0)
    keep_own.wait()
    to_place.wait()
    to_scalar = pltpu.make_async_copy(want_in, sel, loc_sem.at[9])
    to_scalar.start()
    ld_dv.wait()
    ld_rh.wait()
    for q, value in enumerate(solve(0)):
        high = value.astype(jnp.bfloat16)
        low[c * SEG + q] = high
        rest[c * SEG + q] = (value - high.astype(jnp.float32)).astype(jnp.bfloat16)
    hi_out = to_cols(low, hi_s, hi_r, SEG)
    lo_out = to_cols(rest, lo_s, lo_r, SEG)
    for cp in hi_out:
        cp.start()
    to_scalar.wait()
    for d in PEERS:
        from_cols(low, hi_s, hi_r, SEG, d)

    def give(e, carry):
        peer = lax.rem(r + e, NR)
        a2a[e] = low[sel[peer, 0, r]]
        remote(a2a.at[e], recent.at[r], a_s.at[e], a_r.at[e], (peer, c)).start()
        return carry

    lax.fori_loop(1, NR, give, 0)
    recent[r] = low[sel[r, 0, r]]
    for cp in lo_out:
        cp.start()

    def take(e, carry):
        slot = recent.at[lax.rem(r + NR - e, NR)]
        remote(slot, slot, a_s.at[e], a_r.at[e], (r, c)).wait_recv()
        return carry

    lax.fori_loop(1, NR, take, 0)

    def late(slots):
        scatter(1, lambda s: part[s] + product(1, s, recent, new_index, slots))

    pl.when(even_col)(lambda: late((0, 2)))
    pl.when(jnp.logical_not(even_col))(lambda: late((1,)))

    for d in PEERS:
        from_cols(rest, lo_s, lo_r, SEG, d)
    out[0] = low[...].astype(jnp.float32) + rest[...].astype(jnp.float32)
    put(fin.at[c], jnp.concatenate(solve(1), axis=0))
    fin_out = to_cols(fin, fin_s, fin_r, 1)
    for cp in fin_out:
        cp.start()

    def show(z):
        value = decode(fin[z, 0:SEG_ROWS], fin[z, SEG_ROWS:CODED])
        out[1, pl.ds(z * SEG, SEG)] = value.reshape(SEG, P_SIZE, B)

    show(c)
    for cp in sends:
        cp.wait_send()
    for cp, h, item in sib:
        cp.wait_send()

    def left(e, carry):
        peer = lax.rem(r + e, NR)
        remote(want, want_in.at[r], w_s.at[e], w_r.at[e], (peer, c)).wait_send()
        remote(a2a.at[e], recent.at[r], a_s.at[e], a_r.at[e], (peer, c)).wait_send()
        return carry

    lax.fori_loop(1, NR, left, 0)
    for d in PEERS:
        code_copy(0, d).wait_send()
        code_copy(1, d).wait_send()
    for cp in hi_out + lo_out:
        cp.wait_send()
    for d in PEERS[::-1]:
        from_cols(fin, fin_s, fin_r, 1, d)
        show(lax.rem(c + NZ - d, NZ))
    for cp in fin_out:
        cp.wait_send()


def shards(owner_map, colidx, live, blocks, diag_inverse, right_side, prior):
    dma = pltpu.SemaphoreType.DMA
    hbm = pl.BlockSpec(memory_space=pltpu.HBM)
    operands = [owner_map, colidx.transpose(2, 0, 1), live, blocks, diag_inverse, right_side, prior]
    operands = [pltpu.with_memory_space_constraint(x, pltpu.HBM) for x in operands]
    return pl.pallas_call(
        kernel,
        out_shape=jax.ShapeDtypeStruct((2, ROWS_DEV, P_SIZE, B), jnp.float32),
        in_specs=[hbm] * 7,
        out_specs=pl.BlockSpec(memory_space=pltpu.VMEM),
        scratch_shapes=[
            pltpu.VMEM((NPRI + 1, P_SIZE, B), jnp.bfloat16),
            pltpu.VMEM((NR + 1, P_SIZE, B), jnp.bfloat16),
            pltpu.VMEM((2, ROWS_DEV, NBC, B, B), jnp.bfloat16),
            pltpu.VMEM((2, SEG, B, B), jnp.float32),
            pltpu.VMEM((2, SEG, P_SIZE, B), jnp.float32),
            pltpu.VMEM((ROWS_DEV, P_SIZE, B), jnp.float32),
            pltpu.VMEM((2, SEG, P_SIZE, B), jnp.float32),
            pltpu.VMEM((2, NZ, CODED, B), jnp.int16),
            pltpu.VMEM((2, NZ, CODED, B), jnp.int16),
            pltpu.VMEM((NZ, CODED, B), jnp.int16),
            pltpu.VMEM((ROWS_DEV, P_SIZE, B), jnp.bfloat16),
            pltpu.VMEM((ROWS_DEV, P_SIZE, B), jnp.bfloat16),
            pltpu.VMEM((NR, P_SIZE, B), jnp.bfloat16),
            pltpu.VMEM((2, ROWS_F), jnp.int32),
            pltpu.VMEM((SLOTS, 1, B), jnp.int32),
            pltpu.VMEM((1, B), jnp.int32),
            pltpu.VMEM((NR, 1, B), jnp.int32),
            pltpu.SMEM((NBC, 2, ROWS_DEV), jnp.int32),
            pltpu.SMEM((2, ROWS_DEV), jnp.int32),
            pltpu.SMEM((SLOTS, 1, B), jnp.int32),
            pltpu.SMEM((NR, 1, B), jnp.int32),
            dma((10,)),
            dma((NR,)), dma((NR,)),
            dma((36,)), dma((64,)),
            dma((32,)), dma((32,)),
            dma((2, NZ)), dma((2, NZ)),
            dma((NZ,)), dma((NZ,)),
            dma((NZ,)), dma((NZ,)),
            dma((NZ,)), dma((NZ,)),
            dma((NR,)), dma((NR,)),
        ],
        compiler_params=pltpu.CompilerParams(
            collective_id=0, has_side_effects=True, vmem_limit_bytes=48 * 1024 * 1024
        ),
    )(*operands)


def solution(mesh):
    placed = (
        P(),
        P(None, "rows", "cols"),
        P(None, "rows"),
        P(None, "rows", "cols", None, None),
        P(None, "rows", None, None),
        P(None, "rows", None, None),
        P("rows", None, None),
    )
    return jax.shard_map(
        shards, mesh=mesh, in_specs=placed, out_specs=P(None, "rows", None, None), check_vma=False
    )
```

```python
import jax
import jax.numpy as jnp
from jax import lax
from jax.experimental import pallas as pl
from jax.experimental.pallas import tpu as pltpu
from jax.sharding import PartitionSpec as P

MESH = pl.DeviceIdType.MESH
NX, NY, NZ = 4, 4, 8
NR = NX * NY * 2
PRI_DEV = 8
HALF = PRI_DEV // 2
NPRI = NR * PRI_DEV
ROWS_DEV = 16
ROWS_F = NR * ROWS_DEV
SEG = ROWS_DEV // NZ
NBC = 3
SLOTS = ROWS_DEV * NBC
P_SIZE, B = 64, 128
POWER_ROWS = 16
CODED = P_SIZE + POWER_ROWS
NT = (((1,), (1,)), ((), ()))
PEERS = (4, 3, 5, 2, 6, 1, 7)


def encode(value):
    top = jnp.maximum(jnp.max(jnp.abs(value), axis=0, keepdims=True), 1e-30)
    power = jnp.ceil(jnp.log2(top) + 0.01)
    fixed = jnp.round(value * jnp.exp2(15.0 - power)).astype(jnp.int32).astype(jnp.int16)
    powers = jnp.broadcast_to(power, (POWER_ROWS, B)).astype(jnp.int32).astype(jnp.int16)
    return fixed, powers


def decode(fixed, powers):
    unit = jnp.exp2(powers.astype(jnp.int32).astype(jnp.float32) - 15.0)
    value = fixed.astype(jnp.int32).astype(jnp.float32).reshape(P_SIZE // POWER_ROWS, POWER_ROWS, B) * unit[None]
    return value.reshape(P_SIZE, B)


def kernel(
    owners, cols, live, blocks, dinv, rhs, prior, out,
    known, recent, blk, dv, rh, part, own, code_s, code_r, fin, low, rest, a2a,
    om, place, want, want_in, col_s, live_s, place_s, sel,
    loc_sem, w_s, w_r, t_s, t_r, sib_s, sib_r, rs_s, rs_r, hi_s, hi_r, lo_s, lo_r, fin_s, fin_r, a_s, a_r,
):
    r = lax.axis_index("rows")
    c = lax.axis_index("cols")
    core = lax.rem(r, 2)
    cx = lax.rem(r // 2, NX)
    cy = r // (2 * NX)

    def rid(y, x, k):
        return (lax.rem(y + 2 * NY, NY) * NX + lax.rem(x + 2 * NX, NX)) * 2 + k

    def remote(src, dst, ss, rr, dev):
        return pltpu.make_async_remote_copy(
            src_ref=src, dst_ref=dst, send_sem=ss, recv_sem=rr, device_id=dev, device_id_type=MESH
        )

    locals_ = [
        pltpu.make_async_copy(src, dst, loc_sem.at[i])
        for i, (src, dst) in enumerate((
            (prior, known.at[pl.ds(r * PRI_DEV, PRI_DEV)]),
            (cols, col_s),
            (owners, om),
            (live, live_s),
            (blocks, blk),
            (dinv.at[:, pl.ds(c * SEG, SEG)], dv),
            (rhs.at[:, pl.ds(c * SEG, SEG)], rh),
        ))
    ]
    for cp in locals_:
        cp.start()
    ld_prior, ld_cols, ld_owners, ld_live, ld_blk, ld_dv, ld_rh = locals_

    barrier = pltpu.get_barrier_semaphore()

    def greet_rows(e, carry):
        pl.semaphore_signal(barrier, inc=1, device_id=(lax.rem(r + e, NR), c), device_id_type=MESH)
        return carry

    def greet_cols(e, carry):
        pl.semaphore_signal(barrier, inc=1, device_id=(r, lax.rem(c + e, NZ)), device_id_type=MESH)
        return carry

    lax.fori_loop(1, NR, greet_rows, 0)
    lax.fori_loop(1, NZ, greet_cols, 0)

    known[NPRI] = jnp.zeros((P_SIZE, B), jnp.bfloat16)
    recent[NR] = jnp.zeros((P_SIZE, B), jnp.bfloat16)

    ld_cols.wait()
    ld_owners.wait()
    ld_live.wait()
    ids = om[0:1, :]
    spots = lax.broadcasted_iota(jnp.int32, (1, ROWS_F), 1)

    def find(s, carry):
        for j in range(NBC):
            row = col_s[j, 1, s] - NPRI
            at = jnp.sum(jnp.where(ids == row, spots + 1, 0), axis=1, keepdims=True)
            place[s * NBC + j] = jnp.broadcast_to(at - 1, (1, B))
        return carry

    lax.fori_loop(0, ROWS_DEV, find, 0)
    to_place = pltpu.make_async_copy(place, place_s, loc_sem.at[7])
    to_place.start()
    lanes = lax.broadcasted_iota(jnp.int32, (SLOTS, 1, B), 2)
    spot = place[...]
    want[...] = jnp.max(jnp.where((spot >> 4) == lanes, spot & 15, 0), axis=0)
    pl.semaphore_wait(barrier, NR - 1 + NZ - 1)
    ld_prior.wait()

    sends = []

    def xy(h, a, b):
        return (a, b) if h == 0 else (b, a)

    def src_rows(h, item, lo, n, k):
        dx, dy = xy(h, *item)
        return known.at[pl.ds(rid(cy - dy, cx - dx, k) * PRI_DEV + h * HALF + lo, n)]

    def recv_id(h, item, q):
        return h * 32 + ((item[0] + 4) % 4) * 8 + ((item[1] + 4) % 4) * 2 + q

    def push(h, item, step, lo=0, n=HALF, q=0):
        rows = src_rows(h, item, lo, n, core)
        dx, dy = xy(h, *step)
        got = recv_id(h, (item[0] + step[0], item[1] + step[1]), q)
        cp = remote(rows, rows, t_s.at[len(sends)], t_r.at[got], (rid(cy + dy, cx + dx, core), c))
        cp.start()
        sends.append(cp)

    def arrive(h, item, lo=0, n=HALF, q=0):
        rows = src_rows(h, item, lo, n, core)
        remote(rows, rows, t_s.at[0], t_r.at[recv_id(h, item, q)], (r, c)).wait_recv()

    sib = []

    def to_sibling(h, item):
        rows = src_rows(h, item, 0, HALF, core)
        i = len(sib)
        cp = remote(rows, rows, sib_s.at[i], sib_r.at[i], (rid(cy, cx, 1 - core), c))
        cp.start()
        sib.append((cp, h, item))

    def spread(h, item):
        push(h, item, (0, 1))
        push(h, item, (0, -1))

    for h in (0, 1):
        push(h, (0, 0), (1, 0))
        push(h, (0, 0), (-1, 0))

    def ask(e, carry):
        peer = lax.rem(r + e, NR)
        remote(want, want_in.at[r], w_s.at[e], w_r.at[e], (peer, c)).start()
        return carry

    lax.fori_loop(1, NR, ask, 0)
    for h in (0, 1):
        push(h, (0, 0), (2, 0))
        spread(h, (0, 0))
    for h in (0, 1):
        to_sibling(h, (0, 0))
    keep_own = pltpu.make_async_copy(want, want_in.at[r], loc_sem.at[8])
    keep_own.start()

    for du in (1, -1):
        for h in (0, 1):
            arrive(h, (du, 0))
            spread(h, (du, 0))
            to_sibling(h, (du, 0))

    def relay(h, du):
        for dv_, lo, q in ((1, 0, 0), (-1, HALF // 2, 1)):
            arrive(h, (du, dv_))
            push(h, (du, dv_), (0, dv_), lo, HALF // 2, q)
            to_sibling(h, (du, dv_))

    for h in (0, 1):
        arrive(h, (2, 0))
        spread(h, (2, 0))
        push(h, (2, 0), (0, 2))
        to_sibling(h, (2, 0))
    for du in (0, 1, -1):
        for h in (0, 1):
            relay(h, du)
    for du in (0, 1, -1):
        for h in (0, 1):
            for q in (0, 1):
                arrive(h, (du, 2), q * HALF // 2, HALF // 2, q)
            to_sibling(h, (du, 2))
    for dv_ in (1, -1, 2):
        for h in (0, 1):
            arrive(h, (2, dv_))
            to_sibling(h, (2, dv_))
    ld_blk.wait()
    for i, (cp, h, item) in enumerate(sib):
        rows = src_rows(h, item, 0, HALF, 1 - core)
        remote(rows, rows, sib_s.at[0], sib_r.at[i], (r, c)).wait_recv()

    def product(f, s, held, index, slots):
        xs = jnp.concatenate([held[index(s, j)] for j in slots], axis=1)
        ws = jnp.concatenate([blk[f, s, j] for j in slots], axis=1)
        return lax.dot_general(xs, ws, NT, preferred_element_type=jnp.float32)

    def old_index(f):
        return lambda s, j: jnp.where(c * NBC + j < live_s[f, s], col_s[j, f, s], NPRI)

    def new_index(s, j):
        return jnp.where(c * NBC + j < live_s[1, s], place_s[s * NBC + j, 0, 0] >> 4, NR)

    part_rows = (pl.ds(0, CODED), pl.ds(CODED, P_SIZE))
    row_at = (pl.ds(0, P_SIZE), pl.ds(CODED, P_SIZE))
    power_at = pl.ds(P_SIZE, POWER_ROWS)

    def code_copy(f, q, d):
        return remote(
            code_s.at[f, d, part_rows[q]], code_r.at[f, d, part_rows[q]],
            rs_s.at[f, q, d], rs_r.at[f, q, d], (r, lax.rem(c + d, NZ)),
        )

    def scatter(f, row):
        for d in PEERS:
            peer = lax.rem(c + d, NZ)
            fixed, powers = encode(jnp.concatenate([row(peer * SEG + q) for q in range(SEG)], axis=0))
            code_s[f, d, row_at[0]] = fixed[:P_SIZE]
            code_s[f, d, power_at] = powers
            code_s[f, d, row_at[1]] = fixed[P_SIZE:]
            code_copy(f, 0, d).start()
        for d in PEERS:
            code_copy(f, 1, d).start()
        for q in range(SEG):
            own[f, q] = row(c * SEG + q)

    def solve(f, q):
        resid = rh[f, q] - own[f, q]
        for d in PEERS:
            code_copy(f, q, d).wait_recv()
            resid = resid - decode(code_r[f, d, row_at[q]], code_r[f, d, power_at])
        return lax.dot_general(
            resid, dv[f, q], NT, precision=lax.Precision.HIGHEST, preferred_element_type=jnp.float32
        )

    def to_cols(ref, ss, rr, q):
        mine = ref.at[c * SEG + q]
        return [remote(mine, mine, ss.at[q, d], rr.at[q, d], (r, lax.rem(c + d, NZ))) for d in PEERS]

    def from_cols(ref, ss, rr, q, d):
        theirs = ref.at[lax.rem(c + NZ - d, NZ) * SEG + q]
        remote(theirs, theirs, ss.at[q, d], rr.at[q, d], (r, c)).wait_recv()

    scatter(0, lambda s: product(0, s, known, old_index(0), (0, 1, 2)))

    even_col = lax.rem(c, 2) == 0

    def early(slots):
        def one(s, carry):
            part[s] = product(1, s, known, old_index(1), slots)
            return carry

        lax.fori_loop(0, ROWS_DEV, one, 0)

    pl.when(even_col)(lambda: early((1,)))
    pl.when(jnp.logical_not(even_col))(lambda: early((0, 2)))

    def asked(e, carry):
        remote(want, want_in.at[lax.rem(r + NR - e, NR)], w_s.at[e], w_r.at[e], (r, c)).wait_recv()
        return carry

    lax.fori_loop(1, NR, asked, 0)
    keep_own.wait()
    to_place.wait()
    to_scalar = pltpu.make_async_copy(want_in, sel, loc_sem.at[9])
    to_scalar.start()
    ld_dv.wait()
    ld_rh.wait()
    hi_out, lo_out, fin_out = [], [], []
    for q in range(SEG):
        value = solve(0, q)
        high = value.astype(jnp.bfloat16)
        low[c * SEG + q] = high
        rest[c * SEG + q] = (value - high.astype(jnp.float32)).astype(jnp.bfloat16)
        new = to_cols(low, hi_s, hi_r, q)
        for cp in new:
            cp.start()
        hi_out += new
        lo_out += to_cols(rest, lo_s, lo_r, q)
    to_scalar.wait()
    for q in range(SEG):
        for d in PEERS:
            from_cols(low, hi_s, hi_r, q, d)

    def give(e, carry):
        peer = lax.rem(r + e, NR)
        a2a[e] = low[sel[peer, 0, r]]
        remote(a2a.at[e], recent.at[r], a_s.at[e], a_r.at[e], (peer, c)).start()
        return carry

    lax.fori_loop(1, NR, give, 0)
    recent[r] = low[sel[r, 0, r]]
    for cp in lo_out:
        cp.start()

    def take(e, carry):
        slot = recent.at[lax.rem(r + NR - e, NR)]
        remote(slot, slot, a_s.at[e], a_r.at[e], (r, c)).wait_recv()
        return carry

    lax.fori_loop(1, NR, take, 0)

    def late(slots):
        scatter(1, lambda s: part[s] + product(1, s, recent, new_index, slots))

    pl.when(even_col)(lambda: late((0, 2)))
    pl.when(jnp.logical_not(even_col))(lambda: late((1,)))

    for q in range(SEG):
        for d in PEERS:
            from_cols(rest, lo_s, lo_r, q, d)
    out[0] = low[...].astype(jnp.float32) + rest[...].astype(jnp.float32)

    def show(row):
        out[1, row] = decode(fin[row, row_at[0]], fin[row, power_at])

    for q in range(SEG):
        fixed, powers = encode(solve(1, q))
        fin[c * SEG + q, row_at[0]] = fixed
        fin[c * SEG + q, power_at] = powers
        new = to_cols(fin, fin_s, fin_r, q)
        for cp in new:
            cp.start()
        fin_out += new
    for q in range(SEG):
        show(c * SEG + q)
    for cp in sends:
        cp.wait_send()
    for cp, h, item in sib:
        cp.wait_send()

    def left(e, carry):
        peer = lax.rem(r + e, NR)
        remote(want, want_in.at[r], w_s.at[e], w_r.at[e], (peer, c)).wait_send()
        remote(a2a.at[e], recent.at[r], a_s.at[e], a_r.at[e], (peer, c)).wait_send()
        return carry

    lax.fori_loop(1, NR, left, 0)
    for d in PEERS:
        for f in (0, 1):
            for q in range(SEG):
                code_copy(f, q, d).wait_send()
    for cp in hi_out + lo_out:
        cp.wait_send()
    for q in range(SEG):
        for d in PEERS[::-1]:
            from_cols(fin, fin_s, fin_r, q, d)
            show(lax.rem(c + NZ - d, NZ) * SEG + q)
    for cp in fin_out:
        cp.wait_send()


def shards(owner_map, colidx, live, blocks, diag_inverse, right_side, prior):
    dma = pltpu.SemaphoreType.DMA
    hbm = pl.BlockSpec(memory_space=pltpu.HBM)
    operands = [owner_map, colidx.transpose(2, 0, 1), live, blocks, diag_inverse, right_side, prior]
    operands = [pltpu.with_memory_space_constraint(x, pltpu.HBM) for x in operands]
    return pl.pallas_call(
        kernel,
        out_shape=jax.ShapeDtypeStruct((2, ROWS_DEV, P_SIZE, B), jnp.float32),
        in_specs=[hbm] * 7,
        out_specs=pl.BlockSpec(memory_space=pltpu.VMEM),
        scratch_shapes=[
            pltpu.VMEM((NPRI + 1, P_SIZE, B), jnp.bfloat16),
            pltpu.VMEM((NR + 1, P_SIZE, B), jnp.bfloat16),
            pltpu.VMEM((2, ROWS_DEV, NBC, B, B), jnp.bfloat16),
            pltpu.VMEM((2, SEG, B, B), jnp.float32),
            pltpu.VMEM((2, SEG, P_SIZE, B), jnp.float32),
            pltpu.VMEM((ROWS_DEV, P_SIZE, B), jnp.float32),
            pltpu.VMEM((2, SEG, P_SIZE, B), jnp.float32),
            pltpu.VMEM((2, NZ, CODED + P_SIZE, B), jnp.int16),
            pltpu.VMEM((2, NZ, CODED + P_SIZE, B), jnp.int16),
            pltpu.VMEM((ROWS_DEV, CODED, B), jnp.int16),
            pltpu.VMEM((ROWS_DEV, P_SIZE, B), jnp.bfloat16),
            pltpu.VMEM((ROWS_DEV, P_SIZE, B), jnp.bfloat16),
            pltpu.VMEM((NR, P_SIZE, B), jnp.bfloat16),
            pltpu.VMEM((2, ROWS_F), jnp.int32),
            pltpu.VMEM((SLOTS, 1, B), jnp.int32),
            pltpu.VMEM((1, B), jnp.int32),
            pltpu.VMEM((NR, 1, B), jnp.int32),
            pltpu.SMEM((NBC, 2, ROWS_DEV), jnp.int32),
            pltpu.SMEM((2, ROWS_DEV), jnp.int32),
            pltpu.SMEM((SLOTS, 1, B), jnp.int32),
            pltpu.SMEM((NR, 1, B), jnp.int32),
            dma((10,)),
            dma((NR,)), dma((NR,)),
            dma((36,)), dma((64,)),
            dma((32,)), dma((32,)),
            dma((2, SEG, NZ)), dma((2, SEG, NZ)),
            dma((SEG, NZ)), dma((SEG, NZ)),
            dma((SEG, NZ)), dma((SEG, NZ)),
            dma((SEG, NZ)), dma((SEG, NZ)),
            dma((NR,)), dma((NR,)),
        ],
        compiler_params=pltpu.CompilerParams(
            collective_id=0, has_side_effects=True, vmem_limit_bytes=48 * 1024 * 1024
        ),
    )(*operands)


def solution(mesh):
    placed = (
        P(),
        P(None, "rows", "cols"),
        P(None, "rows"),
        P(None, "rows", "cols", None, None),
        P(None, "rows", None, None),
        P(None, "rows", None, None),
        P("rows", None, None),
    )
    return jax.shard_map(
        shards, mesh=mesh, in_specs=placed, out_specs=P(None, "rows", None, None), check_vma=False
    )
```

```python
import jax
import jax.numpy as jnp
from jax import lax
from jax.experimental import pallas as pl
from jax.experimental.pallas import tpu as pltpu
from jax.sharding import PartitionSpec as P

MESH = pl.DeviceIdType.MESH
NX, NY, NZ = 4, 4, 8
NR = NX * NY * 2
PRI_DEV = 8
HALF = PRI_DEV // 2
NPRI = NR * PRI_DEV
ROWS_DEV = 16
ROWS_F = NR * ROWS_DEV
SEG = ROWS_DEV // NZ
NBC = 3
SLOTS = ROWS_DEV * NBC
P_SIZE, B = 64, 128
POWER_ROWS = 8
CODED = P_SIZE + POWER_ROWS
NT = (((1,), (1,)), ((), ()))
PEERS = (3, 5, 4, 2, 6, 1, 7)


def encode(value):
    top = jnp.maximum(jnp.max(jnp.abs(value), axis=0, keepdims=True), 1e-30)
    power = jnp.ceil(jnp.log2(top) + 0.01)
    fixed = jnp.round(value * jnp.exp2(15.0 - power)).astype(jnp.int32).astype(jnp.int16)
    powers = jnp.broadcast_to(power, (POWER_ROWS, B)).astype(jnp.int32).astype(jnp.int16)
    return fixed, powers


def decode(fixed, powers):
    unit = jnp.exp2(powers.astype(jnp.int32).astype(jnp.float32) - 15.0)
    value = fixed.astype(jnp.int32).astype(jnp.float32).reshape(P_SIZE // POWER_ROWS, POWER_ROWS, B) * unit[None]
    return value.reshape(P_SIZE, B)


def kernel(
    owners, cols, live, blocks, dinv, rhs, prior, out,
    known, recent, blk, dv, rh, part, own, code_s, code_r, fin, low, rest, a2a,
    om, place, want, want_in, col_s, live_s, place_s, sel,
    loc_sem, w_s, w_r, t_s, t_r, sib_s, sib_r, rs_s, rs_r, hi_s, hi_r, lo_s, lo_r, fin_s, fin_r, a_s, a_r,
):
    r = lax.axis_index("rows")
    c = lax.axis_index("cols")
    core = lax.rem(r, 2)
    cx = lax.rem(r // 2, NX)
    cy = r // (2 * NX)

    def rid(y, x, k):
        return (lax.rem(y + 2 * NY, NY) * NX + lax.rem(x + 2 * NX, NX)) * 2 + k

    def remote(src, dst, ss, rr, dev):
        return pltpu.make_async_remote_copy(
            src_ref=src, dst_ref=dst, send_sem=ss, recv_sem=rr, device_id=dev, device_id_type=MESH
        )

    locals_ = [
        pltpu.make_async_copy(src, dst, loc_sem.at[i])
        for i, (src, dst) in enumerate((
            (prior, known.at[pl.ds(r * PRI_DEV, PRI_DEV)]),
            (cols, col_s),
            (owners, om),
            (live, live_s),
            (blocks, blk),
            (dinv.at[:, pl.ds(c * SEG, SEG)], dv),
            (rhs.at[:, pl.ds(c * SEG, SEG)], rh),
        ))
    ]
    for cp in locals_:
        cp.start()
    ld_prior, ld_cols, ld_owners, ld_live, ld_blk, ld_dv, ld_rh = locals_

    barrier = pltpu.get_barrier_semaphore()

    def greet_rows(e, carry):
        pl.semaphore_signal(barrier, inc=1, device_id=(lax.rem(r + e, NR), c), device_id_type=MESH)
        return carry

    def greet_cols(e, carry):
        pl.semaphore_signal(barrier, inc=1, device_id=(r, lax.rem(c + e, NZ)), device_id_type=MESH)
        return carry

    lax.fori_loop(1, NR, greet_rows, 0)
    lax.fori_loop(1, NZ, greet_cols, 0)

    known[NPRI] = jnp.zeros((P_SIZE, B), jnp.bfloat16)
    recent[NR] = jnp.zeros((P_SIZE, B), jnp.bfloat16)

    ld_cols.wait()
    ld_owners.wait()
    ld_live.wait()
    ids = om[0:1, :]
    spots = lax.broadcasted_iota(jnp.int32, (1, ROWS_F), 1)

    def find(s, carry):
        for j in range(NBC):
            row = col_s[j, 1, s] - NPRI
            at = jnp.sum(jnp.where(ids == row, spots + 1, 0), axis=1, keepdims=True)
            place[s * NBC + j] = jnp.broadcast_to(at - 1, (1, B))
        return carry

    lax.fori_loop(0, ROWS_DEV, find, 0)
    to_place = pltpu.make_async_copy(place, place_s, loc_sem.at[7])
    to_place.start()
    lanes = lax.broadcasted_iota(jnp.int32, (SLOTS, 1, B), 2)
    spot = place[...]
    want[...] = jnp.max(jnp.where((spot >> 4) == lanes, spot & 15, 0), axis=0)
    pl.semaphore_wait(barrier, NR - 1 + NZ - 1)
    ld_prior.wait()

    sends = []

    def xy(h, a, b):
        return (a, b) if h == 0 else (b, a)

    def src_rows(h, item, lo, n, k):
        dx, dy = xy(h, *item)
        return known.at[pl.ds(rid(cy - dy, cx - dx, k) * PRI_DEV + h * HALF + lo, n)]

    def recv_id(h, item, q):
        return h * 32 + ((item[0] + 4) % 4) * 8 + ((item[1] + 4) % 4) * 2 + q

    def push(h, item, step, lo=0, n=HALF, q=0):
        rows = src_rows(h, item, lo, n, core)
        dx, dy = xy(h, *step)
        got = recv_id(h, (item[0] + step[0], item[1] + step[1]), q)
        cp = remote(rows, rows, t_s.at[len(sends)], t_r.at[got], (rid(cy + dy, cx + dx, core), c))
        cp.start()
        sends.append(cp)

    def arrive(h, item, lo=0, n=HALF, q=0):
        rows = src_rows(h, item, lo, n, core)
        remote(rows, rows, t_s.at[0], t_r.at[recv_id(h, item, q)], (r, c)).wait_recv()

    sib = []

    def to_sibling(h, item):
        rows = src_rows(h, item, 0, HALF, core)
        i = len(sib)
        cp = remote(rows, rows, sib_s.at[i], sib_r.at[i], (rid(cy, cx, 1 - core), c))
        cp.start()
        sib.append((cp, h, item))

    def spread(h, item):
        push(h, item, (0, 1))
        push(h, item, (0, -1))

    for h in (0, 1):
        push(h, (0, 0), (1, 0))
        push(h, (0, 0), (-1, 0))

    def ask(e, carry):
        peer = lax.rem(r + e, NR)
        remote(want, want_in.at[r], w_s.at[e], w_r.at[e], (peer, c)).start()
        return carry

    lax.fori_loop(1, NR, ask, 0)
    for h in (0, 1):
        push(h, (0, 0), (2, 0))
        spread(h, (0, 0))
    for h in (0, 1):
        to_sibling(h, (0, 0))
    keep_own = pltpu.make_async_copy(want, want_in.at[r], loc_sem.at[8])
    keep_own.start()

    for du in (1, -1):
        for h in (0, 1):
            arrive(h, (du, 0))
            spread(h, (du, 0))
            to_sibling(h, (du, 0))

    def relay(h, du):
        for dv_, lo, q in ((1, 0, 0), (-1, HALF // 2, 1)):
            arrive(h, (du, dv_))
            push(h, (du, dv_), (0, dv_), lo, HALF // 2, q)
            to_sibling(h, (du, dv_))

    for h in (0, 1):
        arrive(h, (2, 0))
        spread(h, (2, 0))
        push(h, (2, 0), (0, 2))
        to_sibling(h, (2, 0))
    for du in (0, 1, -1):
        for h in (0, 1):
            relay(h, du)
    for du in (0, 1, -1):
        for h in (0, 1):
            for q in (0, 1):
                arrive(h, (du, 2), q * HALF // 2, HALF // 2, q)
            to_sibling(h, (du, 2))
    for dv_ in (1, -1, 2):
        for h in (0, 1):
            arrive(h, (2, dv_))
            to_sibling(h, (2, dv_))
    ld_blk.wait()
    for i, (cp, h, item) in enumerate(sib):
        rows = src_rows(h, item, 0, HALF, 1 - core)
        remote(rows, rows, sib_s.at[0], sib_r.at[i], (r, c)).wait_recv()

    def product(f, s, held, index, slots):
        xs = jnp.concatenate([held[index(s, j)] for j in slots], axis=1)
        ws = jnp.concatenate([blk[f, s, j] for j in slots], axis=1)
        return lax.dot_general(xs, ws, NT, preferred_element_type=jnp.float32)

    def old_index(f):
        return lambda s, j: jnp.where(c * NBC + j < live_s[f, s], col_s[j, f, s], NPRI)

    def new_index(s, j):
        return jnp.where(c * NBC + j < live_s[1, s], place_s[s * NBC + j, 0, 0] >> 4, NR)

    part_rows = (pl.ds(0, CODED), pl.ds(CODED, P_SIZE))
    row_at = (pl.ds(0, P_SIZE), pl.ds(CODED, P_SIZE))
    power_at = pl.ds(P_SIZE, POWER_ROWS)

    def code_copy(f, q, d):
        return remote(
            code_s.at[f, d, part_rows[q]], code_r.at[f, d, part_rows[q]],
            rs_s.at[f, q, d], rs_r.at[f, q, d], (r, lax.rem(c + d, NZ)),
        )

    def scatter(f, row):
        for d in PEERS:
            peer = lax.rem(c + d, NZ)
            fixed, powers = encode(jnp.concatenate([row(peer * SEG + q) for q in range(SEG)], axis=0))
            code_s[f, d, row_at[0]] = fixed[:P_SIZE]
            code_s[f, d, power_at] = powers
            code_s[f, d, row_at[1]] = fixed[P_SIZE:]
            code_copy(f, 0, d).start()
        for d in PEERS:
            code_copy(f, 1, d).start()
        for q in range(SEG):
            own[f, q] = row(c * SEG + q)

    def solve(f, q):
        resid = rh[f, q] - own[f, q]
        for d in PEERS:
            code_copy(f, q, d).wait_recv()
            resid = resid - decode(code_r[f, d, row_at[q]], code_r[f, d, power_at])
        return lax.dot_general(
            resid, dv[f, q], NT, precision=lax.Precision.HIGHEST, preferred_element_type=jnp.float32
        )

    def to_cols(ref, ss, rr, q):
        mine = ref.at[c * SEG + q]
        return [remote(mine, mine, ss.at[q, d], rr.at[q, d], (r, lax.rem(c + d, NZ))) for d in PEERS]

    def from_cols(ref, ss, rr, q, d):
        theirs = ref.at[lax.rem(c + NZ - d, NZ) * SEG + q]
        remote(theirs, theirs, ss.at[q, d], rr.at[q, d], (r, c)).wait_recv()

    scatter(0, lambda s: product(0, s, known, old_index(0), (0, 1, 2)))

    even_col = lax.rem(c, 2) == 0

    def early(slots):
        def one(s, carry):
            part[s] = product(1, s, known, old_index(1), slots)
            return carry

        lax.fori_loop(0, ROWS_DEV, one, 0)

    pl.when(even_col)(lambda: early((1,)))
    pl.when(jnp.logical_not(even_col))(lambda: early((0, 2)))

    def asked(e, carry):
        remote(want, want_in.at[lax.rem(r + NR - e, NR)], w_s.at[e], w_r.at[e], (r, c)).wait_recv()
        return carry

    lax.fori_loop(1, NR, asked, 0)
    keep_own.wait()
    to_place.wait()
    to_scalar = pltpu.make_async_copy(want_in, sel, loc_sem.at[9])
    to_scalar.start()
    ld_dv.wait()
    ld_rh.wait()
    hi_out, lo_out, fin_out = [], [], []
    for q in range(SEG):
        value = solve(0, q)
        high = value.astype(jnp.bfloat16)
        low[c * SEG + q] = high
        rest[c * SEG + q] = (value - high.astype(jnp.float32)).astype(jnp.bfloat16)
        new = to_cols(low, hi_s, hi_r, q)
        for cp in new:
            cp.start()
        hi_out += new
        lo_out += to_cols(rest, lo_s, lo_r, q)
    to_scalar.wait()
    for q in range(SEG):
        for d in PEERS:
            from_cols(low, hi_s, hi_r, q, d)

    def give(e, carry):
        peer = lax.rem(r + e, NR)
        a2a[e] = low[sel[peer, 0, r]]
        remote(a2a.at[e], recent.at[r], a_s.at[e], a_r.at[e], (peer, c)).start()
        return carry

    lax.fori_loop(1, NR, give, 0)
    recent[r] = low[sel[r, 0, r]]
    for cp in lo_out:
        cp.start()

    def take(e, carry):
        slot = recent.at[lax.rem(r + NR - e, NR)]
        remote(slot, slot, a_s.at[e], a_r.at[e], (r, c)).wait_recv()
        return carry

    lax.fori_loop(1, NR, take, 0)

    def late(slots):
        scatter(1, lambda s: part[s] + product(1, s, recent, new_index, slots))

    pl.when(even_col)(lambda: late((0, 2)))
    pl.when(jnp.logical_not(even_col))(lambda: late((1,)))

    for q in range(SEG):
        for d in PEERS:
            from_cols(rest, lo_s, lo_r, q, d)
    out[0] = low[...].astype(jnp.float32) + rest[...].astype(jnp.float32)

    def show(row):
        out[1, row] = decode(fin[row, row_at[0]], fin[row, power_at])

    for q in range(SEG):
        fixed, powers = encode(solve(1, q))
        fin[c * SEG + q, row_at[0]] = fixed
        fin[c * SEG + q, power_at] = powers
        new = to_cols(fin, fin_s, fin_r, q)
        for cp in new:
            cp.start()
        fin_out += new
    for q in range(SEG):
        show(c * SEG + q)
    for cp in sends:
        cp.wait_send()
    for cp, h, item in sib:
        cp.wait_send()

    def left(e, carry):
        peer = lax.rem(r + e, NR)
        remote(want, want_in.at[r], w_s.at[e], w_r.at[e], (peer, c)).wait_send()
        remote(a2a.at[e], recent.at[r], a_s.at[e], a_r.at[e], (peer, c)).wait_send()
        return carry

    lax.fori_loop(1, NR, left, 0)
    for d in PEERS:
        for f in (0, 1):
            for q in range(SEG):
                code_copy(f, q, d).wait_send()
    for cp in hi_out + lo_out:
        cp.wait_send()
    for q in range(SEG):
        for d in PEERS[::-1]:
            from_cols(fin, fin_s, fin_r, q, d)
            show(lax.rem(c + NZ - d, NZ) * SEG + q)
    for cp in fin_out:
        cp.wait_send()


def shards(owner_map, colidx, live, blocks, diag_inverse, right_side, prior):
    dma = pltpu.SemaphoreType.DMA
    hbm = pl.BlockSpec(memory_space=pltpu.HBM)
    operands = [owner_map, colidx.transpose(2, 0, 1), live, blocks, diag_inverse, right_side, prior]
    operands = [pltpu.with_memory_space_constraint(x, pltpu.HBM) for x in operands]
    return pl.pallas_call(
        kernel,
        out_shape=jax.ShapeDtypeStruct((2, ROWS_DEV, P_SIZE, B), jnp.float32),
        in_specs=[hbm] * 7,
        out_specs=pl.BlockSpec(memory_space=pltpu.VMEM),
        scratch_shapes=[
            pltpu.VMEM((NPRI + 1, P_SIZE, B), jnp.bfloat16),
            pltpu.VMEM((NR + 1, P_SIZE, B), jnp.bfloat16),
            pltpu.VMEM((2, ROWS_DEV, NBC, B, B), jnp.bfloat16),
            pltpu.VMEM((2, SEG, B, B), jnp.float32),
            pltpu.VMEM((2, SEG, P_SIZE, B), jnp.float32),
            pltpu.VMEM((ROWS_DEV, P_SIZE, B), jnp.float32),
            pltpu.VMEM((2, SEG, P_SIZE, B), jnp.float32),
            pltpu.VMEM((2, NZ, CODED + P_SIZE, B), jnp.int16),
            pltpu.VMEM((2, NZ, CODED + P_SIZE, B), jnp.int16),
            pltpu.VMEM((ROWS_DEV, CODED, B), jnp.int16),
            pltpu.VMEM((ROWS_DEV, P_SIZE, B), jnp.bfloat16),
            pltpu.VMEM((ROWS_DEV, P_SIZE, B), jnp.bfloat16),
            pltpu.VMEM((NR, P_SIZE, B), jnp.bfloat16),
            pltpu.VMEM((2, ROWS_F), jnp.int32),
            pltpu.VMEM((SLOTS, 1, B), jnp.int32),
            pltpu.VMEM((1, B), jnp.int32),
            pltpu.VMEM((NR, 1, B), jnp.int32),
            pltpu.SMEM((NBC, 2, ROWS_DEV), jnp.int32),
            pltpu.SMEM((2, ROWS_DEV), jnp.int32),
            pltpu.SMEM((SLOTS, 1, B), jnp.int32),
            pltpu.SMEM((NR, 1, B), jnp.int32),
            dma((10,)),
            dma((NR,)), dma((NR,)),
            dma((36,)), dma((64,)),
            dma((32,)), dma((32,)),
            dma((2, SEG, NZ)), dma((2, SEG, NZ)),
            dma((SEG, NZ)), dma((SEG, NZ)),
            dma((SEG, NZ)), dma((SEG, NZ)),
            dma((SEG, NZ)), dma((SEG, NZ)),
            dma((NR,)), dma((NR,)),
        ],
        compiler_params=pltpu.CompilerParams(
            collective_id=0, has_side_effects=True, vmem_limit_bytes=48 * 1024 * 1024
        ),
    )(*operands)


def solution(mesh):
    placed = (
        P(),
        P(None, "rows", "cols"),
        P(None, "rows"),
        P(None, "rows", "cols", None, None),
        P(None, "rows", None, None),
        P(None, "rows", None, None),
        P("rows", None, None),
    )
    return jax.shard_map(
        shards, mesh=mesh, in_specs=placed, out_specs=P(None, "rows", None, None), check_vma=False
    )
```

```python
import jax
import jax.numpy as jnp
from jax import lax
from jax.experimental import pallas as pl
from jax.experimental.pallas import tpu as pltpu
from jax.sharding import PartitionSpec as P

MESH = pl.DeviceIdType.MESH
NX, NY, NZ = 4, 4, 8
NR = NX * NY * 2
PRI_DEV = 8
HALF = PRI_DEV // 2
NPRI = NR * PRI_DEV
ROWS_DEV = 16
ROWS_F = NR * ROWS_DEV
SEG = ROWS_DEV // NZ
NBC = 3
SLOTS = ROWS_DEV * NBC
P_SIZE, B = 64, 128
POWER_ROWS = 8
CODED = P_SIZE + POWER_ROWS
NT = (((1,), (1,)), ((), ()))
PEERS = (3, 5, 4, 2, 6, 1, 7)
GATHER_PEERS = (4, 3, 5, 2, 6, 1, 7)


def encode(value):
    top = jnp.maximum(jnp.max(jnp.abs(value), axis=0, keepdims=True), 1e-30)
    power = jnp.ceil(jnp.log2(top) + 0.01)
    fixed = jnp.round(value * jnp.exp2(15.0 - power)).astype(jnp.int32).astype(jnp.int16)
    powers = jnp.broadcast_to(power, (POWER_ROWS, B)).astype(jnp.int32).astype(jnp.int16)
    return fixed, powers


def decode(fixed, powers):
    unit = jnp.exp2(powers.astype(jnp.int32).astype(jnp.float32) - 15.0)
    value = fixed.astype(jnp.int32).astype(jnp.float32).reshape(P_SIZE // POWER_ROWS, POWER_ROWS, B) * unit[None]
    return value.reshape(P_SIZE, B)


def kernel(
    owners, cols, live, blocks, dinv, rhs, prior, out,
    known, recent, blk, dv, rh, part, own, code_s, code_r, fin, low, rest, a2a,
    om, place, want, want_in, col_s, live_s, place_s, sel,
    loc_sem, w_s, w_r, t_s, t_r, sib_s, sib_r, rs_s, rs_r, hi_s, hi_r, lo_s, lo_r, fin_s, fin_r, a_s, a_r,
):
    r = lax.axis_index("rows")
    c = lax.axis_index("cols")
    core = lax.rem(r, 2)
    cx = lax.rem(r // 2, NX)
    cy = r // (2 * NX)

    def rid(y, x, k):
        return (lax.rem(y + 2 * NY, NY) * NX + lax.rem(x + 2 * NX, NX)) * 2 + k

    def remote(src, dst, ss, rr, dev):
        return pltpu.make_async_remote_copy(
            src_ref=src, dst_ref=dst, send_sem=ss, recv_sem=rr, device_id=dev, device_id_type=MESH
        )

    locals_ = [
        pltpu.make_async_copy(src, dst, loc_sem.at[i])
        for i, (src, dst) in enumerate((
            (prior, known.at[pl.ds(r * PRI_DEV, PRI_DEV)]),
            (cols, col_s),
            (owners, om),
            (live, live_s),
            (blocks, blk),
            (dinv.at[:, pl.ds(c * SEG, SEG)], dv),
            (rhs.at[:, pl.ds(c * SEG, SEG)], rh),
        ))
    ]
    for cp in locals_:
        cp.start()
    ld_prior, ld_cols, ld_owners, ld_live, ld_blk, ld_dv, ld_rh = locals_

    barrier = pltpu.get_barrier_semaphore()

    def greet_rows(e, carry):
        pl.semaphore_signal(barrier, inc=1, device_id=(lax.rem(r + e, NR), c), device_id_type=MESH)
        return carry

    def greet_cols(e, carry):
        pl.semaphore_signal(barrier, inc=1, device_id=(r, lax.rem(c + e, NZ)), device_id_type=MESH)
        return carry

    lax.fori_loop(1, NR, greet_rows, 0)
    lax.fori_loop(1, NZ, greet_cols, 0)

    known[NPRI] = jnp.zeros((P_SIZE, B), jnp.bfloat16)
    recent[NR] = jnp.zeros((P_SIZE, B), jnp.bfloat16)

    ld_cols.wait()
    ld_owners.wait()
    ld_live.wait()
    ids = om[0:1, :]
    spots = lax.broadcasted_iota(jnp.int32, (1, ROWS_F), 1)

    def find(s, carry):
        for j in range(NBC):
            row = col_s[j, 1, s] - NPRI
            at = jnp.sum(jnp.where(ids == row, spots + 1, 0), axis=1, keepdims=True)
            place[s * NBC + j] = jnp.broadcast_to(at - 1, (1, B))
        return carry

    lax.fori_loop(0, ROWS_DEV, find, 0)
    to_place = pltpu.make_async_copy(place, place_s, loc_sem.at[7])
    to_place.start()
    lanes = lax.broadcasted_iota(jnp.int32, (SLOTS, 1, B), 2)
    spot = place[...]
    want[...] = jnp.max(jnp.where((spot >> 4) == lanes, spot & 15, 0), axis=0)
    pl.semaphore_wait(barrier, NR - 1 + NZ - 1)
    ld_prior.wait()

    sends = []

    def xy(h, a, b):
        return (a, b) if h == 0 else (b, a)

    def src_rows(h, item, lo, n, k):
        dx, dy = xy(h, *item)
        return known.at[pl.ds(rid(cy - dy, cx - dx, k) * PRI_DEV + h * HALF + lo, n)]

    def recv_id(h, item, q):
        return h * 32 + ((item[0] + 4) % 4) * 8 + ((item[1] + 4) % 4) * 2 + q

    def push(h, item, step, lo=0, n=HALF, q=0):
        rows = src_rows(h, item, lo, n, core)
        dx, dy = xy(h, *step)
        got = recv_id(h, (item[0] + step[0], item[1] + step[1]), q)
        cp = remote(rows, rows, t_s.at[len(sends)], t_r.at[got], (rid(cy + dy, cx + dx, core), c))
        cp.start()
        sends.append(cp)

    def arrive(h, item, lo=0, n=HALF, q=0):
        rows = src_rows(h, item, lo, n, core)
        remote(rows, rows, t_s.at[0], t_r.at[recv_id(h, item, q)], (r, c)).wait_recv()

    sib = []

    def to_sibling(h, item):
        rows = src_rows(h, item, 0, HALF, core)
        i = len(sib)
        cp = remote(rows, rows, sib_s.at[i], sib_r.at[i], (rid(cy, cx, 1 - core), c))
        cp.start()
        sib.append((cp, h, item))

    def spread(h, item):
        push(h, item, (0, 1))
        push(h, item, (0, -1))

    for h in (0, 1):
        push(h, (0, 0), (1, 0))
        push(h, (0, 0), (-1, 0))

    def ask(e, carry):
        peer = lax.rem(r + e, NR)
        remote(want, want_in.at[r], w_s.at[e], w_r.at[e], (peer, c)).start()
        return carry

    lax.fori_loop(1, NR, ask, 0)
    for h in (0, 1):
        push(h, (0, 0), (2, 0))
        spread(h, (0, 0))
    for h in (0, 1):
        to_sibling(h, (0, 0))
    keep_own = pltpu.make_async_copy(want, want_in.at[r], loc_sem.at[8])
    keep_own.start()

    for du in (1, -1):
        for h in (0, 1):
            arrive(h, (du, 0))
            spread(h, (du, 0))
            to_sibling(h, (du, 0))

    def relay(h, du):
        for dv_, lo, q in ((1, 0, 0), (-1, HALF // 2, 1)):
            arrive(h, (du, dv_))
            push(h, (du, dv_), (0, dv_), lo, HALF // 2, q)
            to_sibling(h, (du, dv_))

    for h in (0, 1):
        arrive(h, (2, 0))
        spread(h, (2, 0))
        push(h, (2, 0), (0, 2))
        to_sibling(h, (2, 0))
    for du in (0, 1, -1):
        for h in (0, 1):
            relay(h, du)
    for du in (0, 1, -1):
        for h in (0, 1):
            for q in (0, 1):
                arrive(h, (du, 2), q * HALF // 2, HALF // 2, q)
            to_sibling(h, (du, 2))
    for dv_ in (1, -1, 2):
        for h in (0, 1):
            arrive(h, (2, dv_))
            to_sibling(h, (2, dv_))
    ld_blk.wait()
    for i, (cp, h, item) in enumerate(sib):
        rows = src_rows(h, item, 0, HALF, 1 - core)
        remote(rows, rows, sib_s.at[0], sib_r.at[i], (r, c)).wait_recv()

    def product(f, s, held, index, slots):
        xs = jnp.concatenate([held[index(s, j)] for j in slots], axis=1)
        ws = jnp.concatenate([blk[f, s, j] for j in slots], axis=1)
        return lax.dot_general(xs, ws, NT, preferred_element_type=jnp.float32)

    def old_index(f):
        return lambda s, j: jnp.where(c * NBC + j < live_s[f, s], col_s[j, f, s], NPRI)

    def new_index(s, j):
        return jnp.where(c * NBC + j < live_s[1, s], place_s[s * NBC + j, 0, 0] >> 4, NR)

    part_rows = (pl.ds(0, CODED), pl.ds(CODED, P_SIZE))
    row_at = (pl.ds(0, P_SIZE), pl.ds(CODED, P_SIZE))
    power_at = pl.ds(P_SIZE, POWER_ROWS)

    def code_copy(f, q, d):
        return remote(
            code_s.at[f, d, part_rows[q]], code_r.at[f, d, part_rows[q]],
            rs_s.at[f, q, d], rs_r.at[f, q, d], (r, lax.rem(c + d, NZ)),
        )

    def scatter(f, row):
        for d in PEERS:
            peer = lax.rem(c + d, NZ)
            fixed, powers = encode(jnp.concatenate([row(peer * SEG + q) for q in range(SEG)], axis=0))
            code_s[f, d, row_at[0]] = fixed[:P_SIZE]
            code_s[f, d, power_at] = powers
            code_s[f, d, row_at[1]] = fixed[P_SIZE:]
            code_copy(f, 0, d).start()
        for d in PEERS:
            code_copy(f, 1, d).start()
        for q in range(SEG):
            own[f, q] = row(c * SEG + q)

    def solve(f, q):
        resid = rh[f, q] - own[f, q]
        for d in PEERS:
            code_copy(f, q, d).wait_recv()
            resid = resid - decode(code_r[f, d, row_at[q]], code_r[f, d, power_at])
        return lax.dot_general(
            resid, dv[f, q], NT, precision=lax.Precision.HIGHEST, preferred_element_type=jnp.float32
        )

    def to_cols(ref, ss, rr, q):
        mine = ref.at[c * SEG + q]
        return [remote(mine, mine, ss.at[q, d], rr.at[q, d], (r, lax.rem(c + d, NZ))) for d in GATHER_PEERS]

    def from_cols(ref, ss, rr, q, d):
        theirs = ref.at[lax.rem(c + NZ - d, NZ) * SEG + q]
        remote(theirs, theirs, ss.at[q, d], rr.at[q, d], (r, c)).wait_recv()

    scatter(0, lambda s: product(0, s, known, old_index(0), (0, 1, 2)))

    even_col = lax.rem(c, 2) == 0

    def early(slots):
        def one(s, carry):
            part[s] = product(1, s, known, old_index(1), slots)
            return carry

        lax.fori_loop(0, ROWS_DEV, one, 0)

    pl.when(even_col)(lambda: early((1,)))
    pl.when(jnp.logical_not(even_col))(lambda: early((0, 2)))

    def asked(e, carry):
        remote(want, want_in.at[lax.rem(r + NR - e, NR)], w_s.at[e], w_r.at[e], (r, c)).wait_recv()
        return carry

    lax.fori_loop(1, NR, asked, 0)
    keep_own.wait()
    to_place.wait()
    to_scalar = pltpu.make_async_copy(want_in, sel, loc_sem.at[9])
    to_scalar.start()
    ld_dv.wait()
    ld_rh.wait()
    hi_out, lo_out, fin_out = [], [], []
    for q in range(SEG):
        value = solve(0, q)
        high = value.astype(jnp.bfloat16)
        low[c * SEG + q] = high
        rest[c * SEG + q] = (value - high.astype(jnp.float32)).astype(jnp.bfloat16)
        new = to_cols(low, hi_s, hi_r, q)
        for cp in new:
            cp.start()
        hi_out += new
        lo_out += to_cols(rest, lo_s, lo_r, q)
    to_scalar.wait()
    for q in range(SEG):
        for d in PEERS:
            from_cols(low, hi_s, hi_r, q, d)

    def give(e, carry):
        peer = lax.rem(r + e, NR)
        a2a[e] = low[sel[peer, 0, r]]
        remote(a2a.at[e], recent.at[r], a_s.at[e], a_r.at[e], (peer, c)).start()
        return carry

    lax.fori_loop(1, NR, give, 0)
    recent[r] = low[sel[r, 0, r]]
    for cp in lo_out:
        cp.start()

    def take(e, carry):
        slot = recent.at[lax.rem(r + NR - e, NR)]
        remote(slot, slot, a_s.at[e], a_r.at[e], (r, c)).wait_recv()
        return carry

    lax.fori_loop(1, NR, take, 0)

    def late(slots):
        scatter(1, lambda s: part[s] + product(1, s, recent, new_index, slots))

    pl.when(even_col)(lambda: late((0, 2)))
    pl.when(jnp.logical_not(even_col))(lambda: late((1,)))

    for q in range(SEG):
        for d in PEERS:
            from_cols(rest, lo_s, lo_r, q, d)
    out[0] = low[...].astype(jnp.float32) + rest[...].astype(jnp.float32)

    def show(row):
        out[1, row] = decode(fin[row, row_at[0]], fin[row, power_at])

    for q in range(SEG):
        fixed, powers = encode(solve(1, q))
        fin[c * SEG + q, row_at[0]] = fixed
        fin[c * SEG + q, power_at] = powers
        new = to_cols(fin, fin_s, fin_r, q)
        for cp in new:
            cp.start()
        fin_out += new
    for q in range(SEG):
        show(c * SEG + q)
    for cp in sends:
        cp.wait_send()
    for cp, h, item in sib:
        cp.wait_send()

    def left(e, carry):
        peer = lax.rem(r + e, NR)
        remote(want, want_in.at[r], w_s.at[e], w_r.at[e], (peer, c)).wait_send()
        remote(a2a.at[e], recent.at[r], a_s.at[e], a_r.at[e], (peer, c)).wait_send()
        return carry

    lax.fori_loop(1, NR, left, 0)
    for d in PEERS:
        for f in (0, 1):
            for q in range(SEG):
                code_copy(f, q, d).wait_send()
    for cp in hi_out + lo_out:
        cp.wait_send()
    for q in range(SEG):
        for d in PEERS[::-1]:
            from_cols(fin, fin_s, fin_r, q, d)
            show(lax.rem(c + NZ - d, NZ) * SEG + q)
    for cp in fin_out:
        cp.wait_send()


def shards(owner_map, colidx, live, blocks, diag_inverse, right_side, prior):
    dma = pltpu.SemaphoreType.DMA
    hbm = pl.BlockSpec(memory_space=pltpu.HBM)
    operands = [owner_map, colidx.transpose(2, 0, 1), live, blocks, diag_inverse, right_side, prior]
    operands = [pltpu.with_memory_space_constraint(x, pltpu.HBM) for x in operands]
    return pl.pallas_call(
        kernel,
        out_shape=jax.ShapeDtypeStruct((2, ROWS_DEV, P_SIZE, B), jnp.float32),
        in_specs=[hbm] * 7,
        out_specs=pl.BlockSpec(memory_space=pltpu.VMEM),
        scratch_shapes=[
            pltpu.VMEM((NPRI + 1, P_SIZE, B), jnp.bfloat16),
            pltpu.VMEM((NR + 1, P_SIZE, B), jnp.bfloat16),
            pltpu.VMEM((2, ROWS_DEV, NBC, B, B), jnp.bfloat16),
            pltpu.VMEM((2, SEG, B, B), jnp.float32),
            pltpu.VMEM((2, SEG, P_SIZE, B), jnp.float32),
            pltpu.VMEM((ROWS_DEV, P_SIZE, B), jnp.float32),
            pltpu.VMEM((2, SEG, P_SIZE, B), jnp.float32),
            pltpu.VMEM((2, NZ, CODED + P_SIZE, B), jnp.int16),
            pltpu.VMEM((2, NZ, CODED + P_SIZE, B), jnp.int16),
            pltpu.VMEM((ROWS_DEV, CODED, B), jnp.int16),
            pltpu.VMEM((ROWS_DEV, P_SIZE, B), jnp.bfloat16),
            pltpu.VMEM((ROWS_DEV, P_SIZE, B), jnp.bfloat16),
            pltpu.VMEM((NR, P_SIZE, B), jnp.bfloat16),
            pltpu.VMEM((2, ROWS_F), jnp.int32),
            pltpu.VMEM((SLOTS, 1, B), jnp.int32),
            pltpu.VMEM((1, B), jnp.int32),
            pltpu.VMEM((NR, 1, B), jnp.int32),
            pltpu.SMEM((NBC, 2, ROWS_DEV), jnp.int32),
            pltpu.SMEM((2, ROWS_DEV), jnp.int32),
            pltpu.SMEM((SLOTS, 1, B), jnp.int32),
            pltpu.SMEM((NR, 1, B), jnp.int32),
            dma((10,)),
            dma((NR,)), dma((NR,)),
            dma((36,)), dma((64,)),
            dma((32,)), dma((32,)),
            dma((2, SEG, NZ)), dma((2, SEG, NZ)),
            dma((SEG, NZ)), dma((SEG, NZ)),
            dma((SEG, NZ)), dma((SEG, NZ)),
            dma((SEG, NZ)), dma((SEG, NZ)),
            dma((NR,)), dma((NR,)),
        ],
        compiler_params=pltpu.CompilerParams(
            collective_id=0, has_side_effects=True, vmem_limit_bytes=48 * 1024 * 1024
        ),
    )(*operands)


def solution(mesh):
    placed = (
        P(),
        P(None, "rows", "cols"),
        P(None, "rows"),
        P(None, "rows", "cols", None, None),
        P(None, "rows", None, None),
        P(None, "rows", None, None),
        P("rows", None, None),
    )
    return jax.shard_map(
        shards, mesh=mesh, in_specs=placed, out_specs=P(None, "rows", None, None), check_vma=False
    )
```
